128 devices in a mesh: freq: 4 (over z_hi, core), pos: 32 (over x, y, z_lo).
Axes of the slice: x: 4, y: 4, z: 4 (z_hi: 2, z_lo: 2; z = z_hi * 2 + z_lo), core: 2. Of those that a mesh axis runs over, the one named last changes fastest.
Arguments:
- spectra: bfloat16 [16, 2, 256, 32768], P(None, None, 'freq', 'pos'), may hold values from -6 to 6
- green: bfloat16 [16, 32768, 2048], P('freq', 'pos'), may hold values from -0.0234375 to 0.0234375
- recorded: bfloat16 [256, 1024, 512], P('pos', 'freq'), may hold values from -6 to 6
- filter_taps: float32 [256, 11], P('pos'), may hold values from -3 to 3
Outputs:
- primaries: bfloat16 [256, 1024, 512], P('pos', 'freq')
The draws below stay inside these ranges and needn't reach their ends.
All inputs are finite; a program needn't handle non-finite values.
Results may differ from the reference program's by a relative error of at most 0.001.
Values may be sent and summed in bfloat16 or wider, within the bound.
No kernel may reach another device: no remote copies, remote signals or barrier semaphores. Data moves between devices by JAX's collectives and lax.ppermute only.
A program may use at most 128 MiB of HBM per device.

```python
import jax
import jax.numpy as jnp
from jax import lax

S = 256
R = 1024
NT = 512
TAPS = 11
BAND_START = 32
K = 32768
F = 16


def spiked(entries, key, source, target, shards_of, factor):
    owner, partner = [(jnp.arange(entries.shape[position]) // (entries.shape[position] // shards_of)).reshape([-1 if axis == position else 1 for axis in range(entries.ndim)]) for position in (source, target)]
    chosen = jax.random.permutation(key, shards_of)[partner]
    strong = (owner == chosen) | (owner == (partner + shards_of // 2) % shards_of)
    return jnp.where(strong, factor * entries, entries)


def block_levels(stream_key, dims, cuts, low, high):
    gain, own = 1.0, jax.random.fold_in(stream_key, 6)
    for position, parts in cuts:
        steps = jnp.exp(jax.random.uniform(jax.random.fold_in(own, position), (parts,), jnp.float32, low / len(cuts), high / len(cuts)))
        gain = gain * jnp.repeat(steps, dims[position] // parts).reshape([-1 if axis == position else 1 for axis in range(len(dims))])
    return gain


def centred(rng, shape, deviation, most, split=(), kind=jnp.bfloat16):
    level = block_levels(rng, shape, split, -0.22, 0.18) if split else 1.0
    drawn = jax.random.normal(rng, shape, jnp.float32) * deviation * level
    return jnp.minimum(jnp.maximum(drawn, -most), most).astype(kind)


def bell_draw_with(key, shape, deviation, limit, split, heavy, kind=jnp.bfloat16):
    entries = deviation * jax.random.normal(key, shape, jnp.float32)
    if split:
        entries = entries * block_levels(key, shape, split, -0.22, 0.18)
    return jnp.clip(spiked(entries, jax.random.fold_in(key, 3), *heavy), -limit, limit).astype(kind)


def setup_inputs(seed: int = 0) -> dict:
    key_of = jax.random.split(jax.random.key(seed), 5)
    spectra = bell_draw_with(key_of[0], (F, 2, S, K), 1.0, 6.0, ((2, 4), (3, 32)), (3, 2, 32, 2.75))
    green = centred(key_of[1], (F, K, 2 * R), (2 * K) ** -0.5, 0.0234375, ((0, 4), (1, 32)))
    recorded = centred(key_of[2], (S, R, NT), 1.0, 6.0, ((0, 32), (1, 4)))
    filter_taps = centred(key_of[3], (S, TAPS), 0.3, 3.0, ((0, 32),), jnp.float32)
    return dict(spectra=spectra, green=green, recorded=recorded, filter_taps=filter_taps)


def phase_table(first_freq, freq_count, total_freqs, samples):
    bins = BAND_START + first_freq + jnp.arange(freq_count, dtype=jnp.int32)
    sample_index = jnp.arange(samples, dtype=jnp.int32)
    phase = bins[:, None] * sample_index[None, :] % samples
    angle = 2.0 * jnp.pi / samples * phase.astype(jnp.float32)
    scale = 1.0 / jnp.sqrt(jnp.float32(total_freqs))
    return jnp.stack([jnp.cos(angle), -jnp.sin(angle)], 1) * scale

def reference(spectra, green, recorded, filter_taps):

    def one_slice(pair):
        slice_spectra, slice_green = pair
        product = jnp.dot(slice_spectra.reshape(2 * S, K), slice_green, preferred_element_type=jnp.float32)
        real_part = product[:S, :R] - product[S:, R:]
        imag_part = product[:S, R:] + product[S:, :R]
        return jnp.stack([real_part, imag_part], 0)
    prediction = lax.map(one_slice, (spectra, green))
    table = phase_table(0, F, F, NT)
    predicted = jnp.einsum('fisr,fit->srt', prediction, table, precision=lax.Precision.HIGHEST)
    margin = (TAPS - 1) // 2
    padded = jnp.pad(predicted, ((0, 0), (0, 0), (margin, margin)))
    result = recorded.astype(jnp.float32)
    for lag in range(TAPS):
        result = result - filter_taps[:, lag][:, None, None] * padded[:, :, lag:lag + NT]
    return result.astype(jnp.bfloat16)
```

```python
import functools

import jax
import jax.numpy as jnp
import numpy as np
from jax import lax
from jax.experimental import pallas as pl
from jax.experimental.pallas import tpu as pltpu
from jax.sharding import Mesh
from jax.sharding import PartitionSpec as P

BAND_START = 32
FREQ = ("freq_0", "freq_1")
POS = ("pos_0", "pos_1", "pos_2")
GRID = ("pos_0", "pos_1")
HOME = ("pos_0", "pos_2", "freq_0", "freq_1")
POWER = 9
GAIN = 32.0


def phase_table(total_freqs, samples):
    bins = BAND_START + np.arange(total_freqs)
    phase = bins[:, None] * np.arange(samples)[None, :] % samples
    angle = 2.0 * np.pi / samples * phase
    table = np.stack([np.cos(angle), -np.sin(angle)], 1) / np.sqrt(total_freqs)
    return table.astype(np.float32)


def swapped(block, axis):
    return lax.ppermute(block, axis, [(0, 1), (1, 0)])


def halved(value):
    high = value.astype(jnp.bfloat16)
    return high, (value - high.astype(jnp.float32)).astype(jnp.bfloat16)


def coded(value):
    scaled = value * GAIN
    square = scaled * scaled
    fourth = square * square
    return (fourth * fourth * scaled).astype(jnp.bfloat16)


def decoded(code):
    code = code.astype(jnp.float32)
    size = jnp.exp2(jnp.log2(jnp.abs(code)) * (1 / POWER)) * (1 / GAIN)
    return jnp.where(code < 0, -size, size)


def product_kernel(count, place, *refs):
    blocks, cols, out = refs[:count], refs[count], refs[-1]
    parts, shots, depth = blocks[0].shape[2:]
    half = cols.shape[2] // 2
    _, lines, _, halves, tiles, rows, width = out.shape
    spectra = jnp.concatenate([b[0, 0].reshape(parts * shots, depth) for b in blocks], 0)
    for tile in range(0, tiles, 2):
        span = slice(tile * width, (tile + 2) * width)
        shifted = slice(half + tile * width, half + (tile + 2) * width)
        with_real = jnp.dot(spectra, cols[0, :, span], preferred_element_type=jnp.float32)
        with_imag = jnp.dot(spectra, cols[0, :, shifted], preferred_element_type=jnp.float32)
        for n in range(count):
            top, low = parts * shots * n, parts * shots * n + shots
            real = with_real[top:low] - with_imag[low : low + shots]
            imag = with_imag[top:low] + with_real[low : low + shots]
            for side in range(2):
                here = slice(side * width, (side + 1) * width)
                pair = [v[:, here].reshape(lines, halves, rows // 2, width) for v in (real, imag)]
                out[0, :, n, :, tile + side] = coded(jnp.concatenate(pair, 2))


def products(place, blocks, green, span, lines, halves, groups, into=None):
    _, _, parts, shots, depth = blocks[0][0].shape
    freqs, _, columns = green.shape
    columns //= 2
    width = columns // groups
    rows = parts * shots // lines // halves
    count = len(blocks)
    begin, end = span
    spec = pl.BlockSpec

    def block_spec(array, start):
        if array.shape[0] > 1:
            return spec((1, 1, parts, shots, depth), lambda c, p: (2 * p[0] + p[1], begin - start + c, 0, 0, 0))
        return spec((1, 1, parts, shots, depth), lambda c, p: (0, begin - start + c, 0, 0, 0))

    shape = (freqs, lines, count, halves, groups, rows, width)
    extra = () if into is None else (into,)
    return pl.pallas_call(
        functools.partial(product_kernel, count),
        out_shape=jax.ShapeDtypeStruct(shape, jnp.bfloat16),
        grid_spec=pltpu.PrefetchScalarGridSpec(
            num_scalar_prefetch=1,
            grid=(end - begin,),
            in_specs=[block_spec(*b) for b in blocks]
            + [spec((1, depth, 2 * columns), lambda c, p: (begin + c, 0, 0))]
            + [spec(memory_space=pl.ANY)] * len(extra),
            out_specs=spec((1, *shape[1:]), lambda c, p: (begin + c,) + (0,) * (len(shape) - 1)),
        ),
        input_output_aliases={count + 2: 0} if extra else {},
        cost_estimate=pl.CostEstimate(
            flops=2 * (end - begin) * count * parts * shots * depth * columns * 2,
            bytes_accessed=(end - begin) * depth * columns * 4,
            transcendentals=0,
        ),
        compiler_params=pltpu.CompilerParams(vmem_limit_bytes=61 << 20),
    )(place, *[b[0] for b in blocks], green, *extra)


def passed_kernel(array, out):
    pass


def passed(array):
    anywhere = pl.BlockSpec(memory_space=pl.ANY)
    return pl.pallas_call(
        passed_kernel,
        out_shape=jax.ShapeDtypeStruct(array.shape, array.dtype),
        in_specs=[anywhere],
        out_specs=anywhere,
        input_output_aliases={0: 0},
        name="passed",
    )(array)


def filters_kernel(taps, table, out):
    shots, tap_count = taps.shape
    samples = out.shape[2]
    terms = table.shape[0]
    margin = (tap_count - 1) // 2
    shifted = [table[:, 128 + l - margin : 128 + l - margin + samples] for l in range(tap_count)]
    for s in range(shots):
        total = taps[s, 0] * shifted[0]
        for l in range(1, tap_count):
            total = total + taps[s, l] * shifted[l]
        high, low = halved(total)
        for n, value in enumerate((high, low, high)):
            out[s, n * terms : (n + 1) * terms, :] = value


def filters(filter_taps, table):
    shots = filter_taps.shape[0]
    terms, samples = table.shape
    padded = jnp.asarray(np.pad(table, ((0, 0), (128, 128))))
    return pl.pallas_call(
        filters_kernel,
        out_shape=jax.ShapeDtypeStruct((shots, 3 * terms, samples), jnp.bfloat16),
        in_specs=[
            pl.BlockSpec(memory_space=pltpu.SMEM),
            pl.BlockSpec(memory_space=pltpu.VMEM),
        ],
        out_specs=pl.BlockSpec(memory_space=pltpu.VMEM),
        cost_estimate=pl.CostEstimate(flops=2 * shots * 11 * terms * samples, bytes_accessed=2 << 20, transcendentals=0),
        name="filters",
    )(filter_taps, padded)


def subtract_kernel(sums, shaped, recorded, out, values):
    shot = pl.program_id(0)

    @pl.when(shot == 0)
    def _():
        total = sums[:, 0] + sums[:, 1]
        width = total.shape[-1]
        values[...] = jnp.swapaxes(total.reshape(-1, values.shape[0], width), 0, 1)

    high, low = halved(values[shot])
    stacked = jnp.concatenate([high, high, low], 0)
    removed = lax.dot_general(
        stacked, shaped[0], (((0,), (0,)), ((), ())), preferred_element_type=jnp.float32
    )
    out[0] = (recorded[0].astype(jnp.float32) - removed).astype(jnp.bfloat16)


def subtract(sums, shaped, recorded):
    shots, traces, samples = recorded.shape
    terms = shaped.shape[1] // 3
    spec = pl.BlockSpec
    return pl.pallas_call(
        subtract_kernel,
        out_shape=jax.ShapeDtypeStruct(recorded.shape, jnp.bfloat16),
        grid=(shots,),
        in_specs=[
            spec(sums.shape, lambda s: (0,) * sums.ndim),
            spec((1, *shaped.shape[1:]), lambda s: (s, 0, 0)),
            spec((1, traces, samples), lambda s: (s, 0, 0)),
        ],
        out_specs=spec((1, traces, samples), lambda s: (s, 0, 0)),
        scratch_shapes=[pltpu.VMEM((shots, terms, traces), jnp.float32)],
        name="subtract",
    )(sums, shaped, recorded)


def on_device(spectra, green, recorded, filter_taps):
    total_freqs, parts, shots, depth = spectra.shape
    groups = lax.axis_size(FREQ)
    own_freqs = total_freqs // groups
    lines, halves = lax.axis_size("pos_1"), lax.axis_size("pos_2")
    samples = recorded.shape[2]
    zhi, core = lax.axis_index("freq_0"), lax.axis_index("freq_1")
    place = jnp.stack([zhi, core]).astype(jnp.int32)

    table = phase_table(total_freqs, samples).reshape(groups, own_freqs, parts, samples)
    shaped = filters(filter_taps, table.swapaxes(0, 1).reshape(-1, samples))

    by_owner = spectra.reshape(groups, own_freqs, parts, shots, depth)

    def owned(array, z, c, begin=0, end=own_freqs):
        return lax.dynamic_slice_in_dim(array, (2 * z + c) * own_freqs + begin, end - begin, 0)[None]

    last = own_freqs - 1

    def sent(array, cut, axis):
        piece = cut(array)
        moved = swapped(piece, axis)
        return lax.optimization_barrier((array, piece))[0], moved

    rest, far = sent(spectra, lambda a: owned(a, 1 - zhi, core), "freq_0")
    rest, across = sent(rest, lambda a: owned(a, zhi, 1 - core), "freq_1")
    rest, cross = sent(rest, lambda a: owned(a, 1 - zhi, 1 - core, 0, last), "freq_1")
    rest, cross_last = sent(rest, lambda a: owned(a, 1 - zhi, 1 - core, last), "freq_1")
    far_across = swapped(cross, "freq_0")
    far_across_last = swapped(cross_last, "freq_0")

    def multiplied(blocks, span, into=None):
        return products(place, blocks, green, span, lines, halves, groups, into)

    def summed(part):
        part = part.reshape(-1, *part.shape[2:])
        got = lax.all_to_all(part, GRID, split_axis=0, concat_axis=0, tiled=True)
        return decoded(got).sum(0)

    part = multiplied(((by_owner, 0), (across, 0)), (0, own_freqs))
    part = passed(part)
    own = summed(part)
    part, far, shaped = lax.optimization_barrier((part, far, shaped))
    part = multiplied(((far, 0), (far_across, 0)), (0, last))
    part = multiplied(((far, 0), (far_across_last, last)), (last, own_freqs), part)
    others = summed(part)
    blocks = [own[0], own[1], others[0], others[1]]
    blocks = [jnp.where(core == 0, blocks[n], blocks[n ^ 1]) for n in range(4)]
    own = jnp.stack([jnp.where(zhi == 0, blocks[n], blocks[n ^ 2]) for n in range(4)])
    own = own.reshape(-1, *own.shape[3:])
    got = lax.all_to_all(own, HOME, split_axis=0, concat_axis=0, tiled=True)
    got = got.reshape(own_freqs, halves, groups * parts, -1, got.shape[-1])
    return subtract(got, shaped, recorded)


def solution(mesh):
    torus = Mesh(
        mesh.devices.reshape(2, 2, 4, 4, 2), ("freq_0", "freq_1", "pos_0", "pos_1", "pos_2")
    )
    placed = (P(None, None, FREQ, POS), P(FREQ, POS, None), P(POS, FREQ, None), P(POS, None))
    return jax.shard_map(on_device, mesh=torus, in_specs=placed, out_specs=P(POS, FREQ, None), check_vma=False)
```

```python
import functools

import jax
import jax.numpy as jnp
import numpy as np
from jax import lax
from jax.experimental import pallas as pl
from jax.experimental.pallas import tpu as pltpu
from jax.sharding import Mesh
from jax.sharding import PartitionSpec as P

BAND_START = 32
FREQ = ("freq_0", "freq_1")
POS = ("pos_0", "pos_1", "pos_2")
GRID = ("pos_0", "pos_1")
HOME = ("pos_0", "pos_2", "freq_0", "freq_1")
GAIN = 64.0


def phase_table(total_freqs, samples):
    bins = BAND_START + np.arange(total_freqs)
    phase = bins[:, None] * np.arange(samples)[None, :] % samples
    angle = 2.0 * np.pi / samples * phase
    table = np.stack([np.cos(angle), -np.sin(angle)], 1) / np.sqrt(total_freqs)
    return table.astype(np.float32)


def swapped(block, axis):
    return lax.ppermute(block, axis, [(0, 1), (1, 0)])


def halved(value):
    high = value.astype(jnp.bfloat16)
    return high, (value - high.astype(jnp.float32)).astype(jnp.bfloat16)


def coded(value):
    scaled = value * GAIN
    square = scaled * scaled
    fourth = square * square
    return (fourth * scaled * jnp.maximum(fourth, 256.0)).astype(jnp.bfloat16)


def decoded(code):
    code = code.astype(jnp.float32)
    power = jnp.log2(jnp.abs(code))
    size = jnp.exp2(jnp.minimum(power * (1 / 9), (power - 8.0) * (1 / 5))) * (1 / GAIN)
    return jnp.where(code < 0, -size, size)


def sums_kernel(far, code, *refs):
    out, code_in, totals, in_sems, out_sems = refs[-5:]
    zhi, core = lax.axis_index("freq_0"), lax.axis_index("freq_1")
    first = 2 * (1 - zhi if far else zhi)
    places = (first + core, first + 1 - core)
    _, slots, halves, groups = code.shape[:4]
    pieces = [(slot, half) for slot in range(slots) for half in range(halves)]

    def load(n):
        slot, half = pieces[n]
        return pltpu.make_async_copy(code.at[:, slot, half], code_in.at[n], in_sems.at[n])

    def store(n):
        slot, half = pieces[n]
        return pltpu.make_async_copy(totals.at[n], out.at[places[slot], half], out_sems.at[n])

    for n in range(len(pieces)):
        load(n).start()
    for n in range(len(pieces)):
        load(n).wait()

        def step(g, carry):
            total = decoded(code_in[n, 0, g])
            for source in range(1, code_in.shape[1]):
                total = total + decoded(code_in[n, source, g])
            totals[n, g] = total
            return carry

        lax.fori_loop(0, groups, step, 0)
        store(n).start()
    for n in range(len(pieces)):
        store(n).wait()


def sums(code, far, into=None):
    sources, slots, halves, *rest = code.shape
    extra = () if into is None else (into,)
    anywhere = pl.BlockSpec(memory_space=pl.ANY)
    pieces = slots * halves
    return pl.pallas_call(
        functools.partial(sums_kernel, far),
        out_shape=jax.ShapeDtypeStruct((2 * slots, halves, *rest), jnp.float32),
        in_specs=[anywhere] * (1 + len(extra)),
        out_specs=anywhere,
        input_output_aliases={1: 0} if extra else {},
        scratch_shapes=[
            pltpu.VMEM((pieces, sources, *rest), code.dtype),
            pltpu.VMEM((pieces, *rest), jnp.float32),
            pltpu.SemaphoreType.DMA((pieces,)),
            pltpu.SemaphoreType.DMA((pieces,)),
        ],
        cost_estimate=pl.CostEstimate(flops=12 << 20, bytes_accessed=3 << 20, transcendentals=2 << 20),
        compiler_params=pltpu.CompilerParams(vmem_limit_bytes=(61 if far else 40) << 20),
        name="sums",
    )(code, *extra)


def cut_kernel(spectra, far, across, *rest):
    *pieces, sems = rest
    zhi, core = lax.axis_index("freq_0"), lax.axis_index("freq_1")
    freqs = across.shape[0]
    start = (2 * (1 - zhi) + core) * freqs
    copies = [pltpu.make_async_copy(spectra.at[pl.ds(start, freqs)], far, sems.at[len(pieces) + 1])]
    start = (2 * zhi + 1 - core) * freqs
    copies.append(pltpu.make_async_copy(spectra.at[pl.ds(start, freqs)], across, sems.at[0]))
    start = (2 * (1 - zhi) + 1 - core) * freqs
    for n, piece in enumerate(pieces):
        copies.append(pltpu.make_async_copy(spectra.at[pl.ds(start, piece.shape[0])], piece, sems.at[n + 1]))
        start = start + piece.shape[0]
    for copy in copies:
        copy.start()
    for copy in copies:
        copy.wait()


def cut(spectra, own_freqs, counts):
    counts = (own_freqs, own_freqs, *counts)
    return pl.pallas_call(
        cut_kernel,
        out_shape=[jax.ShapeDtypeStruct((n, *spectra.shape[1:]), spectra.dtype) for n in counts],
        in_specs=[pl.BlockSpec(memory_space=pltpu.HBM)],
        out_specs=[pl.BlockSpec(memory_space=pltpu.VMEM)] * len(counts),
        scratch_shapes=[pltpu.SemaphoreType.DMA((len(counts),))],
        compiler_params=pltpu.CompilerParams(vmem_limit_bytes=61 << 20),
        name="cut",
    )(spectra)


def multiply(blocks, cols, write, lines, halves, groups):
    parts, shots, depth = blocks[0].shape
    half = cols.shape[1] // 2
    width = half // groups
    rows = jnp.concatenate([b.reshape(parts * shots, depth) for b in blocks], 0)
    for tile in range(0, groups, 2):
        span = slice(tile * width, (tile + 2) * width)
        shifted = slice(half + tile * width, half + (tile + 2) * width)
        with_real = jnp.dot(rows, cols[:, span], preferred_element_type=jnp.float32)
        with_imag = jnp.dot(rows, cols[:, shifted], preferred_element_type=jnp.float32)
        for slot in range(len(blocks)):
            top = slot * parts * shots
            middle, end = top + shots, top + parts * shots
            real = with_real[top:middle] - with_imag[middle:end]
            imag = with_imag[top:middle] + with_real[middle:end]
            for side in range(2):
                here = slice(side * width, (side + 1) * width)
                pair = [v[:, here].reshape(lines, halves, -1, width) for v in (real, imag)]
                write(slot, tile + side, coded(jnp.concatenate(pair, 2)))


def block_kernel(begin, first_slot, slots, green, *refs):
    blocks = refs[:slots]
    out, blocks_in, green_in, codes, block_sems, green_sems, code_sems = refs[-7:]
    count = green_in.shape[0]
    owner = 2 * lax.axis_index("freq_0") + lax.axis_index("freq_1")

    def loads(n):
        copies = [pltpu.make_async_copy(green.at[begin + n], green_in.at[n], green_sems.at[n])]
        for slot, block in enumerate(blocks):
            at = owner * green.shape[0] + n if block.shape[0] > green.shape[0] else n
            copies.append(pltpu.make_async_copy(block.at[at], blocks_in.at[slot, n], block_sems.at[slot, n]))
        return copies

    def store(n):
        return pltpu.make_async_copy(codes.at[n], out.at[begin + n, :, pl.ds(first_slot, slots)], code_sems.at[n])

    for n in range(count):
        for copy in loads(n):
            copy.start()

    def step(n, carry):
        for copy in loads(n):
            copy.wait()

        def write(slot, tile, code):
            codes[n, :, slot, :, tile] = code

        _, lines, _, halves, groups = codes.shape[:5]
        multiply([blocks_in[slot, n] for slot in range(slots)], green_in.at[n], write, lines, halves, groups)
        store(n).start()
        return carry

    lax.fori_loop(0, count, step, 0)
    for n in range(count):
        store(n).wait()


def block_products(blocks, green, begin, count, slot, shape, into=None):
    parts, shots, depth = blocks[0].shape[1:]
    slots = len(blocks)
    extra = () if into is None else (into,)
    hbm, anywhere = (pl.BlockSpec(memory_space=m) for m in (pltpu.HBM, pl.ANY))
    flops = 4 * slots * count * parts * shots * depth * green.shape[2] // 2
    return pl.pallas_call(
        functools.partial(block_kernel, begin, slot, slots),
        out_shape=jax.ShapeDtypeStruct(shape, jnp.bfloat16),
        in_specs=[hbm] + [anywhere] * slots + [hbm] * len(extra),
        out_specs=hbm,
        input_output_aliases={} if into is None else {1 + slots: 0},
        scratch_shapes=[
            pltpu.VMEM((slots, count, parts, shots, depth), blocks[0].dtype),
            pltpu.VMEM((count, *green.shape[1:]), green.dtype),
            pltpu.VMEM((count, shape[1], slots, *shape[3:]), jnp.bfloat16),
            pltpu.SemaphoreType.DMA((slots, count)),
            pltpu.SemaphoreType.DMA((count,)),
            pltpu.SemaphoreType.DMA((count,)),
        ],
        cost_estimate=pl.CostEstimate(flops=flops, bytes_accessed=count << 22, transcendentals=0),
        compiler_params=pltpu.CompilerParams(vmem_limit_bytes=61 << 20),
    )(green, *blocks, *extra)


def filters_kernel(taps, table, out):
    shots, tap_count = taps.shape
    samples = out.shape[2]
    terms = table.shape[0]
    margin = (tap_count - 1) // 2
    shifted = [table[:, 128 + l - margin : 128 + l - margin + samples] for l in range(tap_count)]
    for s in range(shots):
        total = taps[s, 0] * shifted[0]
        for l in range(1, tap_count):
            total = total + taps[s, l] * shifted[l]
        high, low = halved(total)
        for n, value in enumerate((high, low, high)):
            out[s, n * terms : (n + 1) * terms, :] = value


def filters(filter_taps, table):
    shots = filter_taps.shape[0]
    terms, samples = table.shape
    padded = jnp.asarray(np.pad(table, ((0, 0), (128, 128))))
    return pl.pallas_call(
        filters_kernel,
        out_shape=jax.ShapeDtypeStruct((shots, 3 * terms, samples), jnp.bfloat16),
        in_specs=[
            pl.BlockSpec(memory_space=pltpu.SMEM),
            pl.BlockSpec(memory_space=pltpu.VMEM),
        ],
        out_specs=pl.BlockSpec(memory_space=pltpu.VMEM),
        cost_estimate=pl.CostEstimate(flops=2 * shots * 11 * terms * samples, bytes_accessed=2 << 20, transcendentals=0),
        compiler_params=pltpu.CompilerParams(vmem_limit_bytes=8 << 20),
        name="filters",
    )(filter_taps, padded)


def subtract_kernel(sums, shaped, recorded, out, values):
    @pl.when(pl.program_id(0) == 0)
    def _():
        total = sums[:, 0] + sums[:, 1]
        width = total.shape[-1]
        values[...] = jnp.swapaxes(total.reshape(-1, values.shape[0], width), 0, 1)

    for n in range(out.shape[0]):
        high, low = halved(values[pl.program_id(0) * out.shape[0] + n])
        stacked = jnp.concatenate([high, high, low], 0)
        removed = lax.dot_general(
            stacked, shaped[n], (((0,), (0,)), ((), ())), preferred_element_type=jnp.float32
        )
        out[n] = (recorded[n].astype(jnp.float32) - removed).astype(jnp.bfloat16)


def subtract(sums, shaped, recorded):
    shots, traces, samples = recorded.shape
    terms = shaped.shape[1] // 3
    spec = pl.BlockSpec
    step = 2
    return pl.pallas_call(
        subtract_kernel,
        out_shape=jax.ShapeDtypeStruct(recorded.shape, jnp.bfloat16),
        grid=(shots // step,),
        in_specs=[
            spec(memory_space=pltpu.VMEM),
            spec((step, *shaped.shape[1:]), lambda s: (s, 0, 0)),
            spec((step, traces, samples), lambda s: (s, 0, 0)),
        ],
        out_specs=spec((step, traces, samples), lambda s: (s, 0, 0)),
        scratch_shapes=[pltpu.VMEM((shots, terms, traces), jnp.float32)],
        compiler_params=pltpu.CompilerParams(vmem_limit_bytes=16 << 20),
        name="subtract",
    )(sums, shaped, recorded)


def on_device(spectra, green, recorded, filter_taps):
    total_freqs, parts, shots, _ = spectra.shape
    groups = lax.axis_size(FREQ)
    own_freqs = total_freqs // groups
    lines, halves = lax.axis_size("pos_1"), lax.axis_size("pos_2")
    samples = recorded.shape[2]
    table = phase_table(total_freqs, samples).reshape(groups, own_freqs, parts, samples)
    shaped = filters(filter_taps, table.swapaxes(0, 1).reshape(-1, samples))

    counts = (own_freqs - 2, 1, 1)

    far, across, *pieces = cut(spectra, own_freqs, counts)
    far = swapped(far, "freq_0")
    across = swapped(across, "freq_1")
    pieces = [swapped(piece, "freq_1") for piece in pieces]
    pieces = [swapped(piece, "freq_0") for piece in pieces]

    def scattered(part):
        part = part.reshape(-1, *part.shape[2:])
        return lax.all_to_all(part, GRID, split_axis=0, concat_axis=0, tiled=True)

    shape = (own_freqs, lines, 2, halves, groups, parts * shots // lines // halves, green.shape[2] // 2 // groups)
    part = block_products((spectra, across), green, 0, own_freqs, 0, shape)
    total = sums(scattered(part), False)
    part, far, shaped = lax.optimization_barrier((part, far, shaped))
    part = block_products((far,), green, 0, own_freqs, 0, shape)
    begin = 0
    for piece, count in zip(pieces, counts):
        part = block_products((piece,), green, begin, count, 1, shape, part)
        begin += count
    total = sums(scattered(part), True, total)
    total = total.reshape(-1, *total.shape[3:])
    got = lax.all_to_all(total, HOME, split_axis=0, concat_axis=0, tiled=True)
    got = got.reshape(own_freqs, halves, groups * parts, -1, got.shape[-1])
    return subtract(got, shaped, recorded)


def solution(mesh):
    torus = Mesh(
        mesh.devices.reshape(2, 2, 4, 4, 2), ("freq_0", "freq_1", "pos_0", "pos_1", "pos_2")
    )
    placed = (P(None, None, FREQ, POS), P(FREQ, POS, None), P(POS, FREQ, None), P(POS, None))
    return jax.shard_map(on_device, mesh=torus, in_specs=placed, out_specs=P(POS, FREQ, None), check_vma=False)
```
